128 devices in a mesh: node: 16 (over x, y), local: 8 (over z, core).
Axes of the slice: x: 4, y: 4, z: 4, core: 2. Of those that a mesh axis runs over, the one named last changes fastest.
Arguments:
- tokens: bfloat16 [16384, 4096], P(('node', 'local')), may hold values from -6 to 6
- routes: int32 [16384, 8], P(('node', 'local')), may hold values from 0 to 127, all different within a row; in each aligned block of 128 rows (0 to 127, 128 to 255, ...) at most 10 rows name the same one
- gates: float32 [16384, 8], P(('node', 'local')), may hold values from 0.05 to 1
- placement: int32 [128], replicated, may hold values from 0 to 127, each once
- w_gate: bfloat16 [128, 4096, 768], P(('node', 'local')), may hold values from -0.09375 to 0.09375
- w_up: bfloat16 [128, 4096, 768], P(('node', 'local')), may hold values from -0.09375 to 0.09375
- w_down: bfloat16 [128, 768, 4096], P(('node', 'local')), may hold values from -0.21875 to 0.21875
Outputs:
- mixed: bfloat16 [16384, 4096], P(('node', 'local'))
The draws below stay inside these ranges and needn't reach their ends.
Inputs may be any that keep to these rules, and one draw needn't show every extreme that they name: `routes`: in each block of 128 rows no expert is named more than 10 times, some expert exactly 10 times; a row never names an expert twice. `placement`: every slot holds exactly one expert.
All inputs are finite; a program needn't handle non-finite values.
Results may differ from the reference program's by a relative error of at most 0.008.
Values may be sent and summed in bfloat16 or wider, within the bound.
No kernel may reach another device: no remote copies, remote signals or barrier semaphores. Data moves between devices by JAX's collectives and lax.ppermute only.
A program may use at most 128 MiB of HBM per device.

```python
import math
import jax
import jax.numpy as jnp
import numpy as np
from jax import lax

D = 4096
HID = 768
TOP = 8
TOK_DEV = 128
EXPERTS = 128
CAP = 10
TOKENS = 16384


def shard_levels(stream_key, extent, pieces, least, high):
    def one(position, parts):
        draws = jax.random.uniform(jax.random.fold_in(jax.random.fold_in(stream_key, 6), position), (parts,), jnp.float32, least / len(pieces), high / len(pieces))
        return jnp.repeat(jnp.exp(draws), extent[position] // parts).reshape((-1,) + (1,) * (len(extent) - position - 1))

    gain = one(*pieces[0])
    for cut in pieces[1:]:
        gain = gain * one(*cut)
    return gain


def shared_out(key, own, number, rows, number_of, top, reach, lean):
    ranking = jax.random.permutation(key, number_of)
    packed, common = portions_of(number_of, rows * top, reach, lean, True), portions_of(number_of, rows * top, reach, lean, False)
    places = jnp.arange(number_of)

    def named(tallies, offset_by):
        used = int((tallies > 0).sum())
        fixed = max(1, used // 4)
        moved = fixed + (places - fixed + offset_by * (used - fixed)) % max(1, number_of - fixed)
        return jnp.zeros((number_of,), jnp.int32).at[ranking[jnp.where(places < fixed, places, moved)]].set(jnp.asarray(tallies, jnp.int32))

    tallies = jnp.where(number % 4 == 0, named(packed, number // 4), named(common, number - number // 4 - 1))
    mixed = jax.random.permutation(jax.random.fold_in(own, 3), number_of)
    donor, sink = mixed[0:number_of // 2 * 2:2], mixed[1:number_of // 2 * 2:2]
    slack = jnp.minimum(tallies[donor] - 1, reach - tallies[sink]) // 2
    slack = jnp.where((donor == ranking[0]) | (sink == ranking[0]) | (tallies[sink] == 0), 0, jnp.maximum(slack, 0))
    moved = jax.random.randint(jax.random.fold_in(own, 4), (number_of // 2,), 0, 1 << 20) % (slack + 1)
    tallies = tallies.at[donor].add(-moved).at[sink].add(moved)
    labels = jnp.searchsorted(jnp.cumsum(tallies), jnp.arange(rows * top), side="right").astype(jnp.int32)
    grid = labels.reshape(top, rows).T
    grid = grid[jax.random.permutation(jax.random.fold_in(own, 1), rows)]
    offset_by = jax.random.randint(jax.random.fold_in(own, 2), (rows, 1), 0, top)
    return jnp.take_along_axis(grid, (jnp.arange(top)[None, :] + offset_by) % top, axis=1)


def portions_of(count, total, most, slope, full):
    portions = [(1 << 20) // math.isqrt(rank ** slope) + 1 for rank in range(1, count + 1)]
    largest = most if full else min(most, max(-(-total // count), total * portions[0] // sum(portions)))
    least = 1 if total - largest >= count - 1 else 0
    counts, surplus = [largest] + [least] * (count - 1), total - largest - least * (count - 1)
    while surplus > 0:
        candidates = [i for i in range(1, count) if counts[i] < largest] or [i for i in range(1, count) if counts[i] < most]
        pool, remaining = sum([portions[i] for i in candidates]), surplus
        for i in candidates:
            more = min(most - counts[i], max(1, remaining * portions[i] // pool), surplus)
            counts[i] = counts[i] + more
            surplus = surplus - more
    return np.array(counts)


def gaussian(rng, extent, width, reach, shards=(), kind=jnp.bfloat16):
    level = shard_levels(rng, extent, shards, -0.22, 0.18) if shards else 1.0
    result = jax.random.normal(rng, extent, jnp.float32) * width * level
    return jnp.minimum(jnp.maximum(result, -reach), reach).astype(kind)


def setup_inputs(seed: int = 0) -> dict:
    streams_of = jax.random.split(jax.random.key(seed), 8)
    tokens = gaussian(streams_of[0], (TOKENS, D), 1.0, 6.0, ((0, 128),))
    routes_keys = jax.random.split(jax.random.fold_in(streams_of[1], 1), TOKENS // TOK_DEV)
    routes_turns = jax.random.permutation(jax.random.fold_in(streams_of[1], 3), TOKENS // TOK_DEV)
    routes = jax.vmap(lambda own, number: shared_out(jax.random.fold_in(streams_of[1], 2), own, number, TOK_DEV, EXPERTS, TOP, CAP, 2))(routes_keys, routes_turns).reshape((TOKENS, TOP))
    gates = jnp.clip(jnp.exp(math.log(1.0) - 2.9957323 * jax.random.uniform(streams_of[2], (TOKENS, TOP), jnp.float32) ** shard_levels(streams_of[2], (TOKENS, TOP), ((0, 128),), -0.2, 0.2)), 0.05, 1.0)
    placement = jax.random.permutation(streams_of[3], EXPERTS).astype(jnp.int32)
    w_gate = gaussian(streams_of[4], (EXPERTS, D, HID), D ** -0.5, 0.09375, ((0, 128),))
    w_up = gaussian(streams_of[5], (EXPERTS, D, HID), D ** -0.5, 0.09375, ((0, 128),))
    w_down = gaussian(streams_of[6], (EXPERTS, HID, D), HID ** -0.5, 0.21875, ((0, 128),))
    return {"tokens": tokens, "routes": routes, "gates": gates, "placement": placement, "w_gate": w_gate, "w_up": w_up, "w_down": w_down}


def expert_ffn(rows, gate_w, up_w, down_w):
    gate = jnp.dot(rows, gate_w, preferred_element_type=jnp.float32)
    up = jnp.dot(rows, up_w, preferred_element_type=jnp.float32)
    hidden = (jax.nn.silu(gate) * up).astype(jnp.bfloat16)
    return jnp.dot(hidden, down_w, preferred_element_type=jnp.float32).astype(jnp.bfloat16)


def reference(tokens, routes, gates, placement, w_gate, w_up, w_down):
    blocks = TOKENS // TOK_DEV
    pairs = TOK_DEV * TOP
    flat_e = routes.reshape(blocks, pairs)
    onehot = (flat_e[:, :, None] == jnp.arange(EXPERTS, dtype=jnp.int32)[None, None, :]).astype(jnp.int32)
    rank = jnp.sum(jnp.cumsum(onehot, axis=1) * onehot, axis=2) - 1
    home = placement[flat_e]
    dest = (home * CAP + rank).astype(jnp.int32)

    def table(dest_row):
        return jnp.full((EXPERTS * CAP,), -1, jnp.int32).at[dest_row].set(jnp.arange(pairs, dtype=jnp.int32))

    tab = jax.vmap(table)(dest).reshape(blocks, EXPERTS, CAP)
    tab = jnp.transpose(tab, (1, 0, 2)).reshape(EXPERTS, blocks * CAP)
    source = jnp.repeat(jnp.arange(blocks, dtype=jnp.int32), CAP)
    gate_flat = gates.reshape(-1)

    def step(total, item):
        entry, gate_w, up_w, down_w = item
        valid = entry >= 0
        safe = jnp.maximum(entry, 0)
        token_id = (source * TOK_DEV + safe // TOP).astype(jnp.int32)
        pair_id = (source * pairs + safe).astype(jnp.int32)
        rows = jnp.where(valid[:, None], tokens[token_id], jnp.zeros((), jnp.bfloat16))
        out_rows = expert_ffn(rows, gate_w, up_w, down_w)
        weight = jnp.where(valid, gate_flat[pair_id], jnp.float32(0.0))
        total = total.at[token_id].add(weight[:, None] * out_rows.astype(jnp.float32))
        return total, None

    start = jnp.zeros((TOKENS, D), jnp.float32)
    total, unused = lax.scan(step, start, (tab, w_gate, w_up, w_down))
    return total.astype(jnp.bfloat16)
```

```python
import functools

import jax
import jax.numpy as jnp
from jax import lax
from jax.experimental import pallas as pl
from jax.experimental.pallas import tpu as pltpu
from jax.sharding import PartitionSpec as P

AXES = ("node", "local")
F32 = jnp.float32
BF16 = jnp.bfloat16
VMEM_BYTES = 60 << 20


def iota(shape, dim):
    return lax.broadcasted_iota(jnp.int32, shape, dim)


def dot(a, b):
    return jnp.dot(a, b, preferred_element_type=F32)


def rank_by_slot(routes_t, place_row):
    top, tok = routes_t.shape
    slots = place_row.shape[1]
    rows = iota((slots, tok), 0)
    chosen = jnp.zeros((slots, tok), F32)
    for k in range(top):
        chosen = chosen + (routes_t[k : k + 1, :] == rows).astype(F32)
    perm = (place_row == iota((slots, slots), 0)).astype(F32).astype(BF16)
    at_slot = dot(perm, chosen.astype(BF16))
    before = (iota((tok, tok), 0) < iota((tok, tok), 1)).astype(F32).astype(BF16)
    rank = dot(at_slot.astype(BF16), before)
    return jnp.where(at_slot > 0.5, rank, -1.0)


def pack_main_kernel(routes_ref, place_ref, tok_ref, out_ref, key_ref, sel_ref):
    slots, tok = key_ref.shape

    @pl.when(pl.program_id(0) == 0)
    def _():
        key = rank_by_slot(routes_ref[...], place_ref[...])
        key_ref[...] = key
        hit = key[:, None, :] == iota((slots, 8, tok), 1).astype(F32)
        sel_ref[...] = hit.astype(F32).reshape(slots * 8, tok).astype(BF16)

    out_ref[...] = dot(sel_ref[...], tok_ref[...]).astype(BF16)


def pack_over_kernel(key_ref, tok_ref, out_ref):
    slots, tok = key_ref.shape
    wide = out_ref.shape[1]
    key = jnp.broadcast_to(key_ref[...][:, None, :], (slots, 8, tok))
    j = iota((slots, 8, tok), 1)
    hit = key == (8 + j % 2).astype(F32)
    total = None
    for q in range(4):
        sel = (hit & (j // 2 == q)).astype(F32).reshape(slots * 8, tok).astype(BF16)
        part = dot(sel, tok_ref[:, q * wide : (q + 1) * wide])
        total = part if total is None else total + part
    out_ref[...] = total.astype(BF16)


def silu_mul(gate, up):
    return (gate / (1.0 + jnp.exp(-gate)) * up).astype(BF16)


def ffn_main_kernel(x_ref, wg_ref, wu_ref, wd_ref, out_ref, gate_ref, up_ref, hid_ref):
    step = pl.program_id(0)
    rows = x_ref.shape[0]
    block = 256

    def project(first):
        for m in range(0, rows, block):
            ms = slice(m, m + block)
            x = x_ref[ms, :]
            gate = dot(x, wg_ref[0])
            up = dot(x, wu_ref[0])
            if not first:
                gate = gate + gate_ref[ms, :]
                up = up + up_ref[ms, :]
            gate_ref[ms, :] = gate
            up_ref[ms, :] = up

    @pl.when(step == 0)
    def _():
        project(True)

    @pl.when((step > 0) & (step < 4))
    def _():
        project(False)

    @pl.when(step == 4)
    def _():
        for m in range(0, rows, block):
            ms = slice(m, m + block)
            hid_ref[ms, :] = silu_mul(gate_ref[ms, :], up_ref[ms, :])

    @pl.when(step >= 4)
    def _():
        for m in range(0, rows, block):
            out = dot(hid_ref[m : m + block, :], wd_ref[0])
            out_ref[m // 8 : (m + block) // 8] = out.reshape(block // 8, 8, out.shape[1]).astype(BF16)


def ffn_over_kernel(buf_ref, x_ref, wg_ref, wu_ref, wd_ref, out_ref, wide_ref, gate_ref, up_ref, hid_ref):
    del buf_ref
    step = pl.program_id(0)
    slots = out_ref.shape[0]
    width = out_ref.shape[2]

    @pl.when(step == 0)
    def _():
        for c in range(width // 128):
            wide_ref[c] = x_ref[:, c * 128 : (c + 1) * 128].astype(F32)
        gate_ref[...] = jnp.zeros_like(gate_ref)
        up_ref[...] = jnp.zeros_like(up_ref)

    for q in range(4):

        @pl.when(step == q)
        def _(q=q):
            x = jnp.concatenate(
                [
                    jnp.concatenate(
                        [wide_ref[c, pl.ds(2 * q + r, slots, stride=8), :].astype(BF16) for c in range(width // 128)],
                        axis=1,
                    )
                    for r in range(2)
                ],
                axis=0,
            )
            gate_ref[...] += dot(x, wg_ref[0])
            up_ref[...] += dot(x, wu_ref[0])

    @pl.when(step == 4)
    def _():
        hid_ref[...] = silu_mul(gate_ref[...], up_ref[...])

    for q in range(4):

        @pl.when(step == 4 + q)
        def _(q=q):
            out = dot(hid_ref[...], wd_ref[0])
            for r in range(2):
                for c in range(width // 128):
                    wide_ref[c, pl.ds(2 * q + r, slots, stride=8), :] = out[
                        r * slots : (r + 1) * slots, c * 128 : (c + 1) * 128
                    ]

    @pl.when(step == 7)
    def _():
        for c in range(width // 128):
            out_ref[:, :, c * 128 : (c + 1) * 128] = wide_ref[c].reshape(slots, 8, 128).astype(BF16)


def combine_kernel(routes_ref, gates_ref, place_ref, main_ref, over_ref, out_ref, cmain_ref, cover_ref):
    tok, top = routes_ref.shape
    slots = place_ref.shape[0]
    q = pl.program_id(0)

    @pl.when((q == 0) & (pl.program_id(1) == 0))
    def _():
        lanes = iota((tok, slots), 1)
        chosen = jnp.zeros((tok, slots), F32)
        weight = jnp.zeros((tok, slots), F32)
        for k in range(top):
            hit = (routes_ref[:, k : k + 1] == lanes).astype(F32)
            chosen = chosen + hit
            weight = weight + hit * gates_ref[:, k : k + 1]
        perm = (place_ref[...] == iota((slots, slots), 1)).astype(F32).astype(BF16)
        high = weight.astype(BF16)
        low = (weight - high.astype(F32)).astype(BF16)
        at_slot = dot(chosen.astype(BF16), perm)
        before = (iota((tok, tok), 1) < iota((tok, tok), 0)).astype(F32).astype(BF16)
        rank = dot(before, at_slot.astype(BF16))
        key = jnp.where(at_slot > 0.5, rank, -1.0).astype(BF16)
        spread = (iota((slots, slots * 8), 1) // 8 == iota((slots, slots * 8), 0)).astype(F32).astype(BF16)
        key = dot(key, spread)
        high = dot(dot(high, perm).astype(BF16), spread)
        low = dot(dot(low, perm).astype(BF16), spread)
        j = iota((tok, slots * 8), 1) % 8
        hit = key == j.astype(F32)
        cmain_ref[:tok, :] = jnp.where(hit, high, 0.0).astype(BF16)
        cmain_ref[tok:, :] = jnp.where(hit, low, 0.0).astype(BF16)
        hit = key == (8 + j % 2).astype(F32)
        for p in range(4):
            here = hit & (j // 2 == p)
            cover_ref[p, :tok, :] = jnp.where(here, high, 0.0).astype(BF16)
            cover_ref[p, tok:, :] = jnp.where(here, low, 0.0).astype(BF16)

    rows = slots * 8
    wide = out_ref.shape[1]
    total = dot(cmain_ref[...], main_ref[...].reshape(rows, wide))
    total = total + dot(cover_ref[q], over_ref[...].reshape(rows, wide))
    out_ref[...] = (total[:tok] + total[tok:]).astype(BF16)


def params(grid_dims):
    return pltpu.CompilerParams(dimension_semantics=("arbitrary",) * grid_dims, vmem_limit_bytes=VMEM_BYTES)


def shape(dims, kind=BF16):
    return jax.ShapeDtypeStruct(dims, kind)


def on_device(tokens, routes, gates, placement, w_gate, w_up, w_down):
    tok, width = tokens.shape
    slots = placement.shape[0]
    hid = w_gate.shape[2]
    rows = slots * 8
    wide = width // 4
    exchange = functools.partial(lax.all_to_all, axis_name=AXES, split_axis=0, concat_axis=0, tiled=True)
    whole = lambda *dims: pl.BlockSpec(dims, lambda *_: (0,) * len(dims))

    main, key = pl.pallas_call(
        pack_main_kernel,
        name="pack_main",
        grid=(4,),
        in_specs=[whole(routes.shape[1], tok), whole(1, slots), pl.BlockSpec((tok, wide), lambda i: (0, i))],
        out_specs=[pl.BlockSpec((rows, wide), lambda i: (0, i)), whole(slots, tok)],
        out_shape=[shape((rows, width)), shape((slots, tok), F32)],
        scratch_shapes=[pltpu.VMEM((rows, tok), BF16)],
        compiler_params=params(1),
    )(routes.T, placement.reshape(1, slots), tokens)
    over = pl.pallas_call(
        pack_over_kernel,
        name="pack_over",
        grid=(1,),
        in_specs=[whole(slots, tok), whole(tok, width)],
        out_specs=whole(rows, wide),
        out_shape=shape((rows, wide)),
        compiler_params=params(1),
    )(key, tokens)

    main = exchange(main.reshape(slots, 8, width)).reshape(rows, width)
    over = exchange(over.reshape(slots, 8, wide)).reshape(rows, wide)

    early = lambda i: jnp.minimum(i, 3)
    late = lambda i: jnp.maximum(i - 4, 0)
    weights = [
        pl.BlockSpec((1, wide, hid), lambda i: (0, early(i), 0)),
        pl.BlockSpec((1, wide, hid), lambda i: (0, early(i), 0)),
        pl.BlockSpec((1, hid, wide), lambda i: (0, 0, late(i))),
    ]
    buf = pl.pallas_call(
        ffn_main_kernel,
        name="ffn_main",
        grid=(8,),
        in_specs=[pl.BlockSpec((rows, wide), lambda i: (0, early(i)))] + weights,
        out_specs=pl.BlockSpec((slots, 8, wide), lambda i: (0, late(i), 0)),
        out_shape=shape((slots, 40, wide)),
        scratch_shapes=[pltpu.VMEM((rows, hid), F32), pltpu.VMEM((rows, hid), F32), pltpu.VMEM((rows, hid), BF16)],
        compiler_params=params(1),
    )(main, w_gate, w_up, w_down)
    buf = pl.pallas_call(
        ffn_over_kernel,
        name="ffn_over",
        grid=(8,),
        in_specs=[pl.BlockSpec(memory_space=pl.ANY), whole(rows, wide)] + weights,
        out_specs=pl.BlockSpec((slots, 8, wide), lambda i: (0, 4, 0)),
        out_shape=shape((slots, 40, wide)),
        scratch_shapes=[
            pltpu.VMEM((wide // 128, rows, 128), F32),
            pltpu.VMEM((2 * slots, hid), F32),
            pltpu.VMEM((2 * slots, hid), F32),
            pltpu.VMEM((2 * slots, hid), BF16),
        ],
        input_output_aliases={0: 0},
        compiler_params=params(1),
    )(buf, over, w_gate, w_up, w_down)
    back = exchange(buf)

    half = wide // 2
    return pl.pallas_call(
        combine_kernel,
        name="combine",
        grid=(4, 2),
        in_specs=[
            whole(tok, routes.shape[1]),
            whole(tok, routes.shape[1]),
            whole(slots, 1),
            pl.BlockSpec((slots, 8, half), lambda i, h: (0, i, h)),
            pl.BlockSpec((slots, 8, half), lambda i, h: (0, 4, h)),
        ],
        out_specs=pl.BlockSpec((tok, half), lambda i, h: (0, 2 * i + h)),
        out_shape=shape((tok, width)),
        scratch_shapes=[pltpu.VMEM((2 * tok, rows), BF16), pltpu.VMEM((4, 2 * tok, rows), BF16)],
        compiler_params=params(2),
    )(routes, gates, placement.reshape(slots, 1), back, back)


def solution(mesh):
    placed = (
        P(AXES, None),
        P(AXES, None),
        P(AXES, None),
        P(),
        P(AXES, None, None),
        P(AXES, None, None),
        P(AXES, None, None),
    )
    return jax.shard_map(on_device, mesh=mesh, in_specs=placed, out_specs=P(AXES, None), check_vma=False)
```

```python
import functools

import jax
import jax.numpy as jnp
from jax import lax
from jax.experimental import pallas as pl
from jax.experimental.pallas import tpu as pltpu
from jax.sharding import PartitionSpec as P

AXES = ("node", "local")
F32 = jnp.float32
BF16 = jnp.bfloat16


def iota(shape, dim):
    return lax.broadcasted_iota(jnp.int32, shape, dim)


def dot(a, b):
    return jnp.dot(a, b, preferred_element_type=F32)


def rank_by_slot(routes_t, place_row):
    top, tok = routes_t.shape
    slots = place_row.shape[1]
    rows = iota((slots, tok), 0)
    chosen = jnp.zeros((slots, tok), F32)
    for k in range(top):
        chosen = chosen + (routes_t[k : k + 1, :] == rows).astype(F32)
    perm = (place_row == iota((slots, slots), 0)).astype(F32).astype(BF16)
    at_slot = dot(perm, chosen.astype(BF16))
    before = (iota((tok, tok), 0) < iota((tok, tok), 1)).astype(F32).astype(BF16)
    rank = dot(at_slot.astype(BF16), before)
    return jnp.where(at_slot > 0.5, rank, -1.0)


GROUP = 32


def regroup(back):
    size = GROUP * 8
    grouped, plain = iota((size, size), 1 if back else 0), iota((size, size), 0 if back else 1)
    return (plain == grouped % GROUP * 8 + grouped // GROUP).astype(F32).astype(BF16)


def pack_kernel(routes_ref, place_ref, tok_ref, out_ref, key_ref, sel_ref, part_ref):
    step = pl.program_id(0)
    slots, tok = key_ref.shape
    groups = slots // GROUP
    wide = out_ref.shape[2]
    pair = GROUP * 2

    @pl.when(step == 0)
    def _():
        key = rank_by_slot(routes_ref[...], place_ref[...])
        key_ref[...] = key
        hit = key[:, None, :] == iota((slots, 8, tok), 1).astype(F32)
        sel_ref[...] = hit.astype(F32).reshape(slots * 8, tok).astype(BF16)

    for q in range(4):

        @pl.when(step == q)
        def _(q=q):
            out = dot(sel_ref[...], tok_ref[:, q * wide : (q + 1) * wide])
            out_ref[...] = out.reshape(slots, 8, wide).astype(BF16)

    @pl.when(step == 4)
    def _():
        sel = jnp.concatenate(
            [
                (key_ref[g * GROUP : (g + 1) * GROUP, :] == 8.0 + r).astype(F32)
                for g in range(groups)
                for r in range(2)
            ],
            axis=0,
        ).astype(BF16)
        for q in range(4):
            out = dot(sel, tok_ref[:, q * wide : (q + 1) * wide]).astype(BF16)
            for g in range(groups):
                part_ref[g, q * pair : (q + 1) * pair, :] = out[g * pair : (g + 1) * pair]
        order = regroup(True)
        for g in range(groups):
            out = dot(order, part_ref[g])
            out_ref[g * GROUP : (g + 1) * GROUP] = out.reshape(GROUP, 8, wide).astype(BF16)


def silu_mul(gate, up):
    return (gate / (1.0 + jnp.exp(-gate)) * up).astype(BF16)


def ffn_main_kernel(x_ref, wg_ref, wu_ref, wd_ref, out_ref, gate_ref, up_ref, hid_ref):
    step = pl.program_id(0)
    rows, wide = out_ref.shape
    block = 256

    def project(first):
        for m in range(0, rows, block):
            ms = slice(m, m + block)
            x = x_ref[m // 8 : (m + block) // 8].reshape(block, wide)
            gate = dot(x, wg_ref[0])
            up = dot(x, wu_ref[0])
            if not first:
                gate = gate + gate_ref[ms, :]
                up = up + up_ref[ms, :]
            gate_ref[ms, :] = gate
            up_ref[ms, :] = up

    @pl.when(step == 0)
    def _():
        project(True)

    @pl.when((step > 0) & (step < 4))
    def _():
        project(False)

    @pl.when(step == 4)
    def _():
        for m in range(0, rows, block):
            ms = slice(m, m + block)
            hid_ref[ms, :] = silu_mul(gate_ref[ms, :], up_ref[ms, :])

    @pl.when(step >= 4)
    def _():
        for m in range(0, rows, block):
            ms = slice(m, m + block)
            out_ref[ms, :] = dot(hid_ref[ms, :], wd_ref[0]).astype(BF16)


def ffn_over_kernel(x_ref, wg_ref, wu_ref, wd_ref, out_ref, part_ref, gate_ref, up_ref, hid_ref):
    step = pl.program_id(0)
    groups = part_ref.shape[0]
    wide = out_ref.shape[1]
    size = GROUP * 8
    pair = GROUP * 2

    @pl.when(step == 0)
    def _():
        order = regroup(False)
        for g in range(groups):
            x = x_ref[g * GROUP : (g + 1) * GROUP].reshape(size, wide)
            part_ref[g] = dot(order, x).astype(BF16)
        gate_ref[...] = jnp.zeros_like(gate_ref)
        up_ref[...] = jnp.zeros_like(up_ref)

    @pl.when(step < 4)
    def _():
        here = pl.ds(pl.multiple_of(step * pair, pair), pair)
        x = jnp.concatenate([part_ref[g, here, :] for g in range(groups)], axis=0)
        gate_ref[...] += dot(x, wg_ref[0])
        up_ref[...] += dot(x, wu_ref[0])

    @pl.when(step == 4)
    def _():
        hid_ref[...] = silu_mul(gate_ref[...], up_ref[...])

    @pl.when(step >= 4)
    def _():
        here = pl.ds(pl.multiple_of((step - 4) * pair, pair), pair)
        out = dot(hid_ref[...], wd_ref[0]).astype(BF16)
        for g in range(groups):
            part_ref[g, here, :] = out[g * pair : (g + 1) * pair]

    @pl.when(step == 7)
    def _():
        order = regroup(True)
        for g in range(groups):
            out_ref[g * size : (g + 1) * size, :] = dot(order, part_ref[g]).astype(BF16)


def weights_kernel(routes_ref, gates_ref, place_ref, cmain_ref, cover_ref):
    tok, top = routes_ref.shape
    slots = place_ref.shape[0]
    lanes = iota((tok, slots), 1)
    chosen = jnp.zeros((tok, slots), F32)
    weight = jnp.zeros((tok, slots), F32)
    for k in range(top):
        hit = (routes_ref[:, k : k + 1] == lanes).astype(F32)
        chosen = chosen + hit
        weight = weight + hit * gates_ref[:, k : k + 1]
    perm = (place_ref[...] == iota((slots, slots), 1)).astype(F32).astype(BF16)
    high = weight.astype(BF16)
    low = (weight - high.astype(F32)).astype(BF16)
    at_slot = dot(chosen.astype(BF16), perm)
    before = (iota((tok, tok), 1) < iota((tok, tok), 0)).astype(F32).astype(BF16)
    rank = dot(before, at_slot.astype(BF16))
    key = jnp.where(at_slot > 0.5, rank, -1.0).astype(BF16)
    high = dot(high, perm).astype(BF16)
    low = dot(low, perm).astype(BF16)

    def place(out_ref, slot_of, rank_of):
        width = out_ref.shape[1]
        lane = iota((slots, width), 1)
        spread = (slot_of(lane) == iota((slots, width), 0)).astype(F32).astype(BF16)
        hit = dot(key, spread) == rank_of(iota((tok, width), 1)).astype(F32)
        out_ref[:tok, :] = jnp.where(hit, dot(high, spread), 0.0).astype(BF16)
        out_ref[tok:, :] = jnp.where(hit, dot(low, spread), 0.0).astype(BF16)

    place(cmain_ref, lambda i: i // 8, lambda i: i % 8)
    place(cover_ref, lambda i: i // (2 * GROUP) * GROUP + i % GROUP, lambda i: 8 + i // GROUP % 2)


def combine_over_kernel(cover_ref, over_ref, out_ref):
    tok = out_ref.shape[0]
    wide = over_ref.shape[1]
    size = GROUP * 8
    pair = GROUP * 2
    order = regroup(False)
    parts = [
        dot(order, over_ref[i : i + size, :]).astype(BF16) for i in range(0, over_ref.shape[0], size)
    ]
    for q in range(4):
        over = jnp.concatenate([part[q * pair : (q + 1) * pair] for part in parts], axis=0)
        total = dot(cover_ref[...], over)
        out_ref[:, q * wide : (q + 1) * wide] = total[:tok] + total[tok:]


def combine_main_kernel(cmain_ref, main_ref, over_ref, out_ref):
    tok = out_ref.shape[0]
    total = dot(cmain_ref[...], main_ref[...])
    out_ref[...] = (total[:tok] + total[tok:] + over_ref[...]).astype(BF16)


def params(grid_dims, mib=60):
    return pltpu.CompilerParams(dimension_semantics=("arbitrary",) * grid_dims, vmem_limit_bytes=mib << 20)


def shape(dims, kind=BF16):
    return jax.ShapeDtypeStruct(dims, kind)


def on_device(tokens, routes, gates, placement, w_gate, w_up, w_down):
    tok, width = tokens.shape
    slots = placement.shape[0]
    hid = w_gate.shape[2]
    rows = slots * 8
    wide = width // 4
    exchange = functools.partial(lax.all_to_all, axis_name=AXES, split_axis=0, concat_axis=0, tiled=True)
    whole = lambda *dims: pl.BlockSpec(dims, lambda *_: (0,) * len(dims))

    sent = pl.pallas_call(
        pack_kernel,
        name="pack",
        grid=(5,),
        in_specs=[whole(routes.shape[1], tok), whole(1, slots), whole(tok, width)],
        out_specs=pl.BlockSpec((slots, 8, wide), lambda i: (0, i, 0)),
        out_shape=shape((slots, 40, wide)),
        scratch_shapes=[
            pltpu.VMEM((slots, tok), F32),
            pltpu.VMEM((rows, tok), BF16),
            pltpu.VMEM((slots // GROUP, 8 * GROUP, wide), BF16),
        ],
        compiler_params=params(1),
    )(routes.T, placement.reshape(1, slots), tokens)
    got = exchange(sent)
    cmain, cover = pl.pallas_call(
        weights_kernel,
        name="weights",
        grid=(1,),
        in_specs=[whole(tok, routes.shape[1]), whole(tok, routes.shape[1]), whole(slots, 1)],
        out_specs=[whole(2 * tok, rows), whole(2 * tok, 2 * slots)],
        out_shape=[shape((2 * tok, rows)), shape((2 * tok, 2 * slots))],
        compiler_params=params(1),
    )(routes, gates, placement.reshape(slots, 1))

    early = lambda i: jnp.minimum(i, 3)
    late = lambda i: jnp.maximum(i - 4, 0)
    weights = [
        pl.BlockSpec((1, wide, hid), lambda i: (0, early(i), 0)),
        pl.BlockSpec((1, wide, hid), lambda i: (0, early(i), 0)),
        pl.BlockSpec((1, hid, wide), lambda i: (0, 0, late(i))),
    ]
    over = pl.pallas_call(
        ffn_over_kernel,
        name="ffn_over",
        grid=(8,),
        in_specs=[pl.BlockSpec((slots, 8, wide), lambda i: (0, 4, 0))] + weights,
        out_specs=whole(rows, wide),
        out_shape=shape((rows, wide)),
        scratch_shapes=[
            pltpu.VMEM((slots // GROUP, 8 * GROUP, wide), BF16),
            pltpu.VMEM((2 * slots, hid), F32),
            pltpu.VMEM((2 * slots, hid), F32),
            pltpu.VMEM((2 * slots, hid), BF16),
        ],
        compiler_params=params(1),
    )(got, w_gate, w_up, w_down)
    over = exchange(over.reshape(slots, 8, wide)).reshape(rows, wide)
    main = pl.pallas_call(
        ffn_main_kernel,
        name="ffn_main",
        grid=(8,),
        in_specs=[pl.BlockSpec((slots, 8, wide), lambda i: (0, early(i), 0))] + weights,
        out_specs=pl.BlockSpec((rows, wide), lambda i: (0, late(i))),
        out_shape=shape((rows, width)),
        scratch_shapes=[pltpu.VMEM((rows, hid), F32), pltpu.VMEM((rows, hid), F32), pltpu.VMEM((rows, hid), BF16)],
        compiler_params=params(1),
    )(got, w_gate, w_up, w_down)
    main = exchange(main.reshape(slots, 8, width)).reshape(rows, width)

    total = pl.pallas_call(
        combine_over_kernel,
        name="combine_over",
        grid=(1,),
        in_specs=[whole(2 * tok, 2 * slots), whole(rows, wide)],
        out_specs=whole(tok, width),
        out_shape=shape((tok, width), F32),
        compiler_params=params(1),
    )(cover, over)
    half = wide // 2
    return pl.pallas_call(
        combine_main_kernel,
        name="combine_main",
        grid=(8,),
        in_specs=[
            whole(2 * tok, rows),
            pl.BlockSpec((rows, half), lambda i: (0, i)),
            pl.BlockSpec((tok, half), lambda i: (0, i)),
        ],
        out_specs=pl.BlockSpec((tok, half), lambda i: (0, i)),
        out_shape=shape((tok, width)),
        compiler_params=params(1),
    )(cmain, main, total)


def solution(mesh):
    placed = (
        P(AXES, None),
        P(AXES, None),
        P(AXES, None),
        P(),
        P(AXES, None, None),
        P(AXES, None, None),
        P(AXES, None, None),
    )
    return jax.shard_map(on_device, mesh=mesh, in_specs=placed, out_specs=P(AXES, None), check_vma=False)
```

```python
import functools

import jax
import jax.numpy as jnp
from jax import lax
from jax.experimental import pallas as pl
from jax.experimental.pallas import tpu as pltpu
from jax.sharding import PartitionSpec as P

AXES = ("node", "local")
F32 = jnp.float32
BF16 = jnp.bfloat16


def iota(shape, dim):
    return lax.broadcasted_iota(jnp.int32, shape, dim)


def dot(a, b):
    return jnp.dot(a, b, preferred_element_type=F32)


def rank_by_slot(routes_t, place_row):
    top, tok = routes_t.shape
    slots = place_row.shape[1]
    rows = iota((slots, tok), 0)
    chosen = jnp.zeros((slots, tok), F32)
    for k in range(top):
        chosen = chosen + (routes_t[k : k + 1, :] == rows).astype(F32)
    perm = (place_row == iota((slots, slots), 0)).astype(F32).astype(BF16)
    at_slot = dot(perm, chosen.astype(BF16))
    before = (iota((tok, tok), 0) < iota((tok, tok), 1)).astype(F32).astype(BF16)
    rank = dot(at_slot.astype(BF16), before)
    return jnp.where(at_slot > 0.5, rank, -1.0)


GROUP = 32


def regroup(back):
    size = GROUP * 8
    grouped, plain = iota((size, size), 1 if back else 0), iota((size, size), 0 if back else 1)
    return (plain == grouped % GROUP * 8 + grouped // GROUP).astype(F32).astype(BF16)


def pack_kernel(routes_ref, place_ref, tok_ref, out_ref, buf_ref, part_ref, sems):
    tok, width = tok_ref.shape
    slots = place_ref.shape[1]
    groups = slots // GROUP
    wide = width // 4
    pair = GROUP * 2
    key = rank_by_slot(routes_ref[...], place_ref[...])
    hit = key[:, None, :] == iota((slots, 8, tok), 1).astype(F32)
    sel = hit.astype(F32).reshape(slots * 8, tok).astype(BF16)
    copies = []

    def send(q, lo, hi, value):
        buf_ref[lo:hi, q * 8 : (q + 1) * 8, :] = value.reshape(hi - lo, 8, wide).astype(BF16)
        here = (slice(lo, hi), slice(q * 8, (q + 1) * 8))
        copy = pltpu.make_async_copy(buf_ref.at[here], out_ref.at[here], sems.at[len(copies)])
        copy.start()
        copies.append(copy)

    half = slots // 2
    for q in range(4):
        for lo in (0, half):
            rows = sel[lo * 8 : (lo + half) * 8]
            send(q, lo, lo + half, dot(rows, tok_ref[:, q * wide : (q + 1) * wide]))
    sel = jnp.concatenate(
        [
            (key[g * GROUP : (g + 1) * GROUP, :] == 8.0 + r).astype(F32)
            for g in range(groups)
            for r in range(2)
        ],
        axis=0,
    ).astype(BF16)
    for q in range(4):
        out = dot(sel, tok_ref[:, q * wide : (q + 1) * wide]).astype(BF16)
        for g in range(groups):
            part_ref[g, q * pair : (q + 1) * pair, :] = out[g * pair : (g + 1) * pair]
    order = regroup(True)
    for g in range(groups):
        send(4, g * GROUP, (g + 1) * GROUP, dot(order, part_ref[g]))
    for copy in copies:
        copy.wait()


def silu_mul(gate, up):
    return (gate / (1.0 + jnp.exp(-gate)) * up).astype(BF16)


class Queue:
    def __init__(self, copies, depth):
        self.copies, self.depth, self.done = copies, depth, 0
        for copy in copies[:depth]:
            copy.start()

    def next(self):
        self.copies[self.done].wait()
        self.done += 1
        if self.done + self.depth <= len(self.copies):
            self.copies[self.done + self.depth - 1].start()


def ffn_main_kernel(
    got_ref,
    wg_hbm,
    wu_hbm,
    wd_hbm,
    out_ref,
    x_ref,
    wg_ref,
    wu_ref,
    wd_ref,
    gate_ref,
    up_ref,
    hid_ref,
    back_ref,
    in_sems,
    out_sems,
):
    rows, width = back_ref.shape
    wide = width // 4
    block = 512
    blocks = [slice(m, m + block) for m in range(0, rows, block)]
    quarters = [slice(q * wide, (q + 1) * wide) for q in range(4)]
    sem = iter(range(16))
    copies = []
    for q, p in enumerate(quarters):
        copies.append(pltpu.make_async_copy(got_ref.at[:, 8 * q : 8 * q + 8, :], x_ref.at[q], in_sems.at[next(sem)]))
        copies.append(pltpu.make_async_copy(wg_hbm.at[0, p, :], wg_ref.at[p, :], in_sems.at[next(sem)]))
        copies.append(pltpu.make_async_copy(wu_hbm.at[0, p, :], wu_ref.at[p, :], in_sems.at[next(sem)]))
    for p in quarters:
        copies.append(pltpu.make_async_copy(wd_hbm.at[0, :, p], wd_ref.at[:, p], in_sems.at[next(sem)]))
    queue = Queue(copies, 5)
    for q, p in enumerate(quarters):
        for _ in range(3):
            queue.next()
        for m in blocks:
            x = x_ref[q, m.start // 8 : m.stop // 8].reshape(block, wide)
            gate = dot(x, wg_ref[p, :])
            up = dot(x, wu_ref[p, :])
            if q:
                gate = gate + gate_ref[m, :]
                up = up + up_ref[m, :]
            if q < 3:
                gate_ref[m, :] = gate
                up_ref[m, :] = up
            else:
                hid_ref[m, :] = silu_mul(gate, up)
    give = []
    for p in quarters:
        queue.next()
        for m in blocks:
            back_ref[m, p] = dot(hid_ref[m, :], wd_ref[:, p]).astype(BF16)
            copy = pltpu.make_async_copy(back_ref.at[m, p], out_ref.at[m, p], out_sems.at[len(give)])
            copy.start()
            give.append(copy)
    for copy in give:
        copy.wait()


def ffn_over_kernel(
    got_ref, wg_hbm, wu_hbm, wd_hbm, out_ref, x_ref, wg_ref, wu_ref, wd_ref, part_ref, back_ref, in_sems, w_sems, out_sems
):
    groups = part_ref.shape[0]
    wide = x_ref.shape[2]
    size = GROUP * 8
    pair = GROUP * 2
    quarters = [slice(q * wide, (q + 1) * wide) for q in range(4)]
    slots = [slice(g * GROUP, (g + 1) * GROUP) for g in range(groups)]
    lines = [slice(g * size, (g + 1) * size) for g in range(groups)]
    take = [pltpu.make_async_copy(got_ref.at[s, 32:40, :], x_ref.at[s], in_sems.at[g]) for g, s in enumerate(slots)]
    give = [pltpu.make_async_copy(back_ref.at[r, :], out_ref.at[r, :], out_sems.at[g]) for g, r in enumerate(lines)]
    gates = [pltpu.make_async_copy(wg_hbm.at[0, p, :], wg_ref.at[p, :], w_sems.at[q]) for q, p in enumerate(quarters)]
    ups = [pltpu.make_async_copy(wu_hbm.at[0, p, :], wu_ref.at[p, :], w_sems.at[4 + q]) for q, p in enumerate(quarters)]
    downs = [pltpu.make_async_copy(wd_hbm.at[0, :, p], wd_ref.at[:, p], w_sems.at[8 + q]) for q, p in enumerate(quarters)]
    queue = Queue(take + [c for pair_of in zip(gates, ups) for c in pair_of] + downs, 5)
    order = regroup(False)
    for g in range(groups):
        queue.next()
        part_ref[g] = dot(order, x_ref[slots[g]].reshape(size, wide)).astype(BF16)
    gate = up = None
    for q, p in enumerate(quarters):
        x = jnp.concatenate([part_ref[g, q * pair : (q + 1) * pair, :] for g in range(groups)], axis=0)
        queue.next()
        one = dot(x, wg_ref[p, :])
        queue.next()
        two = dot(x, wu_ref[p, :])
        gate, up = (one, two) if q == 0 else (gate + one, up + two)
    hidden = silu_mul(gate, up)
    for q, p in enumerate(quarters):
        queue.next()
        out = dot(hidden, wd_ref[:, p]).astype(BF16)
        for g in range(groups):
            part_ref[g, q * pair : (q + 1) * pair, :] = out[g * pair : (g + 1) * pair]
    order = regroup(True)
    for g in range(groups):
        back_ref[lines[g], :] = dot(order, part_ref[g]).astype(BF16)
        give[g].start()
    for copy in give:
        copy.wait()


def weights_kernel(routes_ref, gates_ref, place_ref, cmain_ref, cover_ref):
    tok, top = routes_ref.shape
    slots = place_ref.shape[0]
    lanes = iota((tok, slots), 1)
    chosen = jnp.zeros((tok, slots), F32)
    weight = jnp.zeros((tok, slots), F32)
    for k in range(top):
        hit = (routes_ref[:, k : k + 1] == lanes).astype(F32)
        chosen = chosen + hit
        weight = weight + hit * gates_ref[:, k : k + 1]
    perm = (place_ref[...] == iota((slots, slots), 1)).astype(F32).astype(BF16)
    high = weight.astype(BF16)
    low = (weight - high.astype(F32)).astype(BF16)
    at_slot = dot(chosen.astype(BF16), perm)
    before = (iota((tok, tok), 1) < iota((tok, tok), 0)).astype(F32).astype(BF16)
    rank = dot(before, at_slot.astype(BF16))
    key = jnp.where(at_slot > 0.5, rank, -1.0).astype(BF16)
    high = dot(high, perm).astype(BF16)
    low = dot(low, perm).astype(BF16)

    def place(out_ref, slot_of, rank_of):
        width = out_ref.shape[1]
        lane = iota((slots, width), 1)
        spread = (slot_of(lane) == iota((slots, width), 0)).astype(F32).astype(BF16)
        hit = dot(key, spread) == rank_of(iota((tok, width), 1)).astype(F32)
        out_ref[:tok, :] = jnp.where(hit, dot(high, spread), 0.0).astype(BF16)
        out_ref[tok:, :] = jnp.where(hit, dot(low, spread), 0.0).astype(BF16)

    place(cmain_ref, lambda i: i // 8, lambda i: i % 8)
    place(cover_ref, lambda i: i // (2 * GROUP) * GROUP + i % GROUP, lambda i: 8 + i // GROUP % 2)


def combine_over_kernel(cover_ref, over_ref, out_ref):
    tok = out_ref.shape[0]
    wide = over_ref.shape[1]
    size = GROUP * 8
    pair = GROUP * 2
    order = regroup(False)
    parts = [
        dot(order, over_ref[i : i + size, :]).astype(BF16) for i in range(0, over_ref.shape[0], size)
    ]
    for q in range(4):
        over = jnp.concatenate([part[q * pair : (q + 1) * pair] for part in parts], axis=0)
        total = dot(cover_ref[...], over)
        out_ref[:, q * wide : (q + 1) * wide] = total[:tok] + total[tok:]


COLUMNS = (1024, 1024, 1024, 512, 512)


def combine_main_kernel(
    cmain_hbm, over_hbm, main_ref, out_ref, cmain_ref, over_ref, x_ref, y_ref, in_sems, over_sems, out_sems, cmain_sem
):
    tok = y_ref.shape[0]
    starts = [sum(COLUMNS[:i]) for i in range(len(COLUMNS))]
    parts = [slice(a, a + n) for a, n in zip(starts, COLUMNS)]
    coefs = pltpu.make_async_copy(cmain_hbm, cmain_ref, cmain_sem)
    take = [pltpu.make_async_copy(main_ref.at[:, p], x_ref.at[:, p], in_sems.at[i]) for i, p in enumerate(parts)]
    more = [pltpu.make_async_copy(over_hbm.at[:, p], over_ref.at[:, p], over_sems.at[i]) for i, p in enumerate(parts)]
    give = [pltpu.make_async_copy(y_ref.at[:, p], out_ref.at[:, p], out_sems.at[i]) for i, p in enumerate(parts)]
    queue = Queue([coefs] + [c for pair_of in zip(take, more) for c in pair_of], 5)
    queue.next()
    for i, p in enumerate(parts):
        queue.next()
        total = dot(cmain_ref[...], x_ref[:, p])
        queue.next()
        y_ref[:, p] = (total[:tok] + total[tok:] + over_ref[:, p]).astype(BF16)
        give[i].start()
    for copy in give:
        copy.wait()


def params(grid_dims, mib=60):
    return pltpu.CompilerParams(dimension_semantics=("arbitrary",) * grid_dims if grid_dims else None, vmem_limit_bytes=mib << 20)


def shape(dims, kind=BF16):
    return jax.ShapeDtypeStruct(dims, kind)


def on_device(tokens, routes, gates, placement, w_gate, w_up, w_down):
    tok, width = tokens.shape
    slots = placement.shape[0]
    hid = w_gate.shape[2]
    rows = slots * 8
    wide = width // 4
    exchange = functools.partial(lax.all_to_all, axis_name=AXES, split_axis=0, concat_axis=0, tiled=True)
    whole = lambda *dims: pl.BlockSpec(dims, lambda *_: (0,) * len(dims))

    hbm = pl.BlockSpec(memory_space=pl.ANY)
    sent = pl.pallas_call(
        pack_kernel,
        name="pack",
        grid=(1,),
        in_specs=[whole(routes.shape[1], tok), whole(1, slots), whole(tok, width)],
        out_specs=hbm,
        out_shape=shape((slots, 40, wide)),
        scratch_shapes=[
            pltpu.VMEM((slots, 40, wide), BF16),
            pltpu.VMEM((slots // GROUP, 8 * GROUP, wide), BF16),
            pltpu.SemaphoreType.DMA((8 + slots // GROUP,)),
        ],
        compiler_params=params(0),
    )(routes.T, placement.reshape(1, slots), tokens)
    got = exchange(sent)
    cmain, cover = pl.pallas_call(
        weights_kernel,
        name="weights",
        grid=(1,),
        in_specs=[whole(tok, routes.shape[1]), whole(tok, routes.shape[1]), whole(slots, 1)],
        out_specs=[whole(2 * tok, rows), whole(2 * tok, 2 * slots)],
        out_shape=[shape((2 * tok, rows)), shape((2 * tok, 2 * slots))],
        compiler_params=params(1),
    )(routes, gates, placement.reshape(slots, 1))

    over = pl.pallas_call(
        ffn_over_kernel,
        name="ffn_over",
        in_specs=[hbm] * 4,
        out_specs=hbm,
        out_shape=shape((rows, wide)),
        scratch_shapes=[
            pltpu.VMEM((slots, 8, wide), BF16),
            pltpu.VMEM((width, hid), BF16),
            pltpu.VMEM((width, hid), BF16),
            pltpu.VMEM((hid, width), BF16),
            pltpu.VMEM((slots // GROUP, 8 * GROUP, wide), BF16),
            pltpu.VMEM((rows, wide), BF16),
            pltpu.SemaphoreType.DMA((slots // GROUP,)),
            pltpu.SemaphoreType.DMA((12,)),
            pltpu.SemaphoreType.DMA((slots // GROUP,)),
        ],
        compiler_params=params(0),
    )(got, w_gate, w_up, w_down)
    over = exchange(over.reshape(slots, 8, wide)).reshape(rows, wide)
    main = pl.pallas_call(
        ffn_main_kernel,
        name="ffn_main",
        in_specs=[hbm] * 4,
        out_specs=hbm,
        out_shape=shape((rows, width)),
        scratch_shapes=[
            pltpu.VMEM((4, slots, 8, wide), BF16),
            pltpu.VMEM((width, hid), BF16),
            pltpu.VMEM((width, hid), BF16),
            pltpu.VMEM((hid, width), BF16),
            pltpu.VMEM((rows, hid), F32),
            pltpu.VMEM((rows, hid), F32),
            pltpu.VMEM((rows, hid), BF16),
            pltpu.VMEM((rows, width), BF16),
            pltpu.SemaphoreType.DMA((16,)),
            pltpu.SemaphoreType.DMA((4 * rows // 512,)),
        ],
        compiler_params=params(0),
    )(got, w_gate, w_up, w_down)
    main = exchange(main.reshape(slots, 8, width)).reshape(rows, width)

    total = pl.pallas_call(
        combine_over_kernel,
        name="combine_over",
        grid=(1,),
        in_specs=[whole(2 * tok, 2 * slots), whole(rows, wide)],
        out_specs=whole(tok, width),
        out_shape=shape((tok, width), F32),
        compiler_params=params(1),
    )(cover, over)
    return pl.pallas_call(
        combine_main_kernel,
        name="combine_main",
        in_specs=[hbm] * 3,
        out_specs=hbm,
        out_shape=shape((tok, width)),
        scratch_shapes=[
            pltpu.VMEM((2 * tok, rows), BF16),
            pltpu.VMEM((tok, width), F32),
            pltpu.VMEM((rows, width), BF16),
            pltpu.VMEM((tok, width), BF16),
            pltpu.SemaphoreType.DMA((len(COLUMNS),)),
            pltpu.SemaphoreType.DMA((len(COLUMNS),)),
            pltpu.SemaphoreType.DMA((len(COLUMNS),)),
            pltpu.SemaphoreType.DMA,
        ],
        compiler_params=params(0),
    )(cmain, total, main)


def solution(mesh):
    placed = (
        P(AXES, None),
        P(AXES, None),
        P(AXES, None),
        P(),
        P(AXES, None, None),
        P(AXES, None, None),
        P(AXES, None, None),
    )
    return jax.shard_map(on_device, mesh=mesh, in_specs=placed, out_specs=P(AXES, None), check_vma=False)
```

```python
import functools

import jax
import jax.numpy as jnp
from jax import lax
from jax.experimental import pallas as pl
from jax.experimental.pallas import tpu as pltpu
from jax.sharding import PartitionSpec as P

AXES = ("node", "local")
F32 = jnp.float32
BF16 = jnp.bfloat16


def iota(shape, dim):
    return lax.broadcasted_iota(jnp.int32, shape, dim)


def dot(a, b):
    return jnp.dot(a, b, preferred_element_type=F32)


def rank_by_slot(routes_t, place_row):
    top, tok = routes_t.shape
    slots = place_row.shape[1]
    rows = iota((slots, tok), 0)
    chosen = jnp.zeros((slots, tok), F32)
    for k in range(top):
        chosen = chosen + (routes_t[k : k + 1, :] == rows).astype(F32)
    perm = (place_row == iota((slots, slots), 0)).astype(F32).astype(BF16)
    at_slot = dot(perm, chosen.astype(BF16))
    before = (iota((tok, tok), 0) < iota((tok, tok), 1)).astype(F32).astype(BF16)
    rank = dot(at_slot.astype(BF16), before)
    return jnp.where(at_slot > 0.5, rank, -1.0)


GROUP = 32


def regroup(back):
    size = GROUP * 8
    grouped, plain = iota((size, size), 1 if back else 0), iota((size, size), 0 if back else 1)
    return (plain == grouped % GROUP * 8 + grouped // GROUP).astype(F32).astype(BF16)


def pack_kernel(routes_ref, place_ref, tok_ref, out_ref, part_ref):
    tok, width = tok_ref.shape
    slots = place_ref.shape[1]
    groups = slots // GROUP
    wide = width // 4
    pair = GROUP * 2
    key = rank_by_slot(routes_ref[...], place_ref[...])
    hit = key[:, None, :] == iota((slots, 8, tok), 1).astype(F32)
    sel = hit.astype(F32).reshape(slots * 8, tok).astype(BF16)

    def send(q, lo, hi, value):
        out_ref[lo:hi, q * 8 : (q + 1) * 8, :] = value.reshape(hi - lo, 8, wide).astype(BF16)

    half = slots // 2
    for q in range(4):
        for lo in (0, half):
            rows = sel[lo * 8 : (lo + half) * 8]
            send(q, lo, lo + half, dot(rows, tok_ref[:, q * wide : (q + 1) * wide]))
    sel = jnp.concatenate(
        [
            (key[g * GROUP : (g + 1) * GROUP, :] == 8.0 + r).astype(F32)
            for g in range(groups)
            for r in range(2)
        ],
        axis=0,
    ).astype(BF16)
    for q in range(4):
        out = dot(sel, tok_ref[:, q * wide : (q + 1) * wide]).astype(BF16)
        for g in range(groups):
            part_ref[g, q * pair : (q + 1) * pair, :] = out[g * pair : (g + 1) * pair]
    order = regroup(True)
    for g in range(groups):
        send(4, g * GROUP, (g + 1) * GROUP, dot(order, part_ref[g]))


def silu_mul(gate, up):
    return (gate / (1.0 + jnp.exp(-gate)) * up).astype(BF16)


class Queue:
    def __init__(self, copies, depth):
        self.copies, self.depth, self.done = copies, depth, 0
        for copy in copies[:depth]:
            copy.start()

    def next(self):
        self.copies[self.done].wait()
        self.done += 1
        if self.done + self.depth <= len(self.copies):
            self.copies[self.done + self.depth - 1].start()


def ffn_main_kernel(
    got_ref,
    wg_hbm,
    wu_hbm,
    wd_hbm,
    out_ref,
    x_ref,
    wg_ref,
    wu_ref,
    wd_ref,
    gate_ref,
    up_ref,
    hid_ref,
    back_ref,
    in_sems,
    out_sems,
):
    rows, width = back_ref.shape
    wide = width // 4
    block = 512
    blocks = [slice(m, m + block) for m in range(0, rows, block)]
    quarters = [slice(q * wide, (q + 1) * wide) for q in range(4)]
    sem = iter(range(16))
    copies = []
    for q, p in enumerate(quarters):
        copies.append(pltpu.make_async_copy(got_ref.at[:, 8 * q : 8 * q + 8, :], x_ref.at[q], in_sems.at[next(sem)]))
        copies.append(pltpu.make_async_copy(wg_hbm.at[0, p, :], wg_ref.at[p, :], in_sems.at[next(sem)]))
        copies.append(pltpu.make_async_copy(wu_hbm.at[0, p, :], wu_ref.at[p, :], in_sems.at[next(sem)]))
    for p in quarters:
        copies.append(pltpu.make_async_copy(wd_hbm.at[0, :, p], wd_ref.at[:, p], in_sems.at[next(sem)]))
    queue = Queue(copies, 5)
    for q, p in enumerate(quarters):
        for _ in range(3):
            queue.next()
        for m in blocks:
            x = x_ref[q, m.start // 8 : m.stop // 8].reshape(block, wide)
            gate = dot(x, wg_ref[p, :])
            up = dot(x, wu_ref[p, :])
            if q:
                gate = gate + gate_ref[m, :]
                up = up + up_ref[m, :]
            if q < 3:
                gate_ref[m, :] = gate
                up_ref[m, :] = up
            else:
                hid_ref[m, :] = silu_mul(gate, up)
    give = []
    for p in quarters:
        queue.next()
        for m in blocks:
            back_ref[m, p] = dot(hid_ref[m, :], wd_ref[:, p]).astype(BF16)
            copy = pltpu.make_async_copy(back_ref.at[m, p], out_ref.at[m, p], out_sems.at[len(give)])
            copy.start()
            give.append(copy)
    for copy in give:
        copy.wait()


def ffn_over_kernel(
    got_ref, wg_ref, wu_ref, wd_hbm, out_ref, x_ref, wd_ref, part_ref, back_ref, in_sems, out_sems
):
    groups = part_ref.shape[0]
    wide = x_ref.shape[2]
    size = GROUP * 8
    pair = GROUP * 2
    quarters = [slice(q * wide, (q + 1) * wide) for q in range(4)]
    slots = [slice(g * GROUP, (g + 1) * GROUP) for g in range(groups)]
    lines = [slice(g * size, (g + 1) * size) for g in range(groups)]
    take = [pltpu.make_async_copy(got_ref.at[s, 32:40, :], x_ref.at[s], in_sems.at[g]) for g, s in enumerate(slots)]
    give = [pltpu.make_async_copy(back_ref.at[r, :], out_ref.at[r, :], out_sems.at[g]) for g, r in enumerate(lines)]
    downs = [
        pltpu.make_async_copy(wd_hbm.at[0, :, p], wd_ref.at[:, p], in_sems.at[groups + q]) for q, p in enumerate(quarters)
    ]
    queue = Queue(take + downs, 5)
    order = regroup(False)
    for g in range(groups):
        queue.next()
        part_ref[g] = dot(order, x_ref[slots[g]].reshape(size, wide)).astype(BF16)
    gate = up = None
    for q, p in enumerate(quarters):
        x = jnp.concatenate([part_ref[g, q * pair : (q + 1) * pair, :] for g in range(groups)], axis=0)
        one = dot(x, wg_ref[0, p, :])
        two = dot(x, wu_ref[0, p, :])
        gate, up = (one, two) if q == 0 else (gate + one, up + two)
    hidden = silu_mul(gate, up)
    for q, p in enumerate(quarters):
        queue.next()
        out = dot(hidden, wd_ref[:, p]).astype(BF16)
        for g in range(groups):
            part_ref[g, q * pair : (q + 1) * pair, :] = out[g * pair : (g + 1) * pair]
    order = regroup(True)
    for g in range(groups):
        back_ref[lines[g], :] = dot(order, part_ref[g]).astype(BF16)
        give[g].start()
    for copy in give:
        copy.wait()


def weights_kernel(routes_ref, gates_ref, place_ref, cmain_ref, cover_ref):
    tok, top = routes_ref.shape
    slots = place_ref.shape[0]
    lanes = iota((tok, slots), 1)
    chosen = jnp.zeros((tok, slots), F32)
    weight = jnp.zeros((tok, slots), F32)
    for k in range(top):
        hit = (routes_ref[:, k : k + 1] == lanes).astype(F32)
        chosen = chosen + hit
        weight = weight + hit * gates_ref[:, k : k + 1]
    perm = (place_ref[...] == iota((slots, slots), 1)).astype(F32).astype(BF16)
    high = weight.astype(BF16)
    low = (weight - high.astype(F32)).astype(BF16)
    at_slot = dot(chosen.astype(BF16), perm)
    before = (iota((tok, tok), 1) < iota((tok, tok), 0)).astype(F32).astype(BF16)
    rank = dot(before, at_slot.astype(BF16))
    key = jnp.where(at_slot > 0.5, rank, -1.0).astype(BF16)
    high = dot(high, perm).astype(BF16)
    low = dot(low, perm).astype(BF16)

    def place(out_ref, slot_of, rank_of):
        width = out_ref.shape[1]
        lane = iota((slots, width), 1)
        spread = (slot_of(lane) == iota((slots, width), 0)).astype(F32).astype(BF16)
        hit = dot(key, spread) == rank_of(iota((tok, width), 1)).astype(F32)
        out_ref[:tok, :] = jnp.where(hit, dot(high, spread), 0.0).astype(BF16)
        out_ref[tok:, :] = jnp.where(hit, dot(low, spread), 0.0).astype(BF16)

    place(cmain_ref, lambda i: i // 8, lambda i: i % 8)
    place(cover_ref, lambda i: i // (2 * GROUP) * GROUP + i % GROUP, lambda i: 8 + i // GROUP % 2)


def combine_over_kernel(cover_ref, over_ref, out_ref):
    tok = out_ref.shape[0]
    wide = over_ref.shape[1]
    size = GROUP * 8
    pair = GROUP * 2
    order = regroup(False)
    parts = [
        dot(order, over_ref[i : i + size, :]).astype(BF16) for i in range(0, over_ref.shape[0], size)
    ]
    for q in range(4):
        over = jnp.concatenate([part[q * pair : (q + 1) * pair] for part in parts], axis=0)
        total = dot(cover_ref[...], over)
        out_ref[:, q * wide : (q + 1) * wide] = total[:tok] + total[tok:]


COLUMNS = (1024, 1024, 1024, 512, 512)


def combine_main_kernel(
    cmain_hbm, over_hbm, main_ref, out_ref, cmain_ref, over_ref, x_ref, y_ref, in_sems, over_sems, out_sems, cmain_sem
):
    tok = y_ref.shape[0]
    starts = [sum(COLUMNS[:i]) for i in range(len(COLUMNS))]
    parts = [slice(a, a + n) for a, n in zip(starts, COLUMNS)]
    coefs = pltpu.make_async_copy(cmain_hbm, cmain_ref, cmain_sem)
    take = [pltpu.make_async_copy(main_ref.at[:, p], x_ref.at[:, p], in_sems.at[i]) for i, p in enumerate(parts)]
    more = [pltpu.make_async_copy(over_hbm.at[:, p], over_ref.at[:, p], over_sems.at[i]) for i, p in enumerate(parts)]
    give = [pltpu.make_async_copy(y_ref.at[:, p], out_ref.at[:, p], out_sems.at[i]) for i, p in enumerate(parts)]
    queue = Queue([coefs] + [c for pair_of in zip(take, more) for c in pair_of], 5)
    queue.next()
    for i, p in enumerate(parts):
        queue.next()
        total = dot(cmain_ref[...], x_ref[:, p])
        queue.next()
        y_ref[:, p] = (total[:tok] + total[tok:] + over_ref[:, p]).astype(BF16)
        give[i].start()
    for copy in give:
        copy.wait()


def params(grid_dims, mib=60):
    return pltpu.CompilerParams(dimension_semantics=("arbitrary",) * grid_dims if grid_dims else None, vmem_limit_bytes=mib << 20)


def shape(dims, kind=BF16):
    return jax.ShapeDtypeStruct(dims, kind)


def on_device(tokens, routes, gates, placement, w_gate, w_up, w_down):
    tok, width = tokens.shape
    slots = placement.shape[0]
    hid = w_gate.shape[2]
    rows = slots * 8
    wide = width // 4
    exchange = functools.partial(lax.all_to_all, axis_name=AXES, split_axis=0, concat_axis=0, tiled=True)
    whole = lambda *dims: pl.BlockSpec(dims, lambda *_: (0,) * len(dims))

    hbm = pl.BlockSpec(memory_space=pl.ANY)
    vmem = pl.BlockSpec(memory_space=pltpu.VMEM)
    sent = pl.pallas_call(
        pack_kernel,
        name="pack",
        in_specs=[vmem, vmem, vmem],
        out_specs=vmem,
        out_shape=pltpu.VMEM((slots, 40, wide), BF16),
        scratch_shapes=[pltpu.VMEM((slots // GROUP, 8 * GROUP, wide), BF16)],
        compiler_params=params(0, 48),
    )(routes.T, placement.reshape(1, slots), tokens)
    got = exchange(sent)
    cmain, cover = pl.pallas_call(
        weights_kernel,
        name="weights",
        grid=(1,),
        in_specs=[whole(tok, routes.shape[1]), whole(tok, routes.shape[1]), whole(slots, 1)],
        out_specs=[whole(2 * tok, rows), whole(2 * tok, 2 * slots)],
        out_shape=[shape((2 * tok, rows)), shape((2 * tok, 2 * slots))],
        compiler_params=params(1),
    )(routes, gates, placement.reshape(slots, 1))

    over = pl.pallas_call(
        ffn_over_kernel,
        name="ffn_over",
        in_specs=[hbm, vmem, vmem, hbm],
        out_specs=hbm,
        out_shape=shape((rows, wide)),
        scratch_shapes=[
            pltpu.VMEM((slots, 8, wide), BF16),
            pltpu.VMEM((hid, width), BF16),
            pltpu.VMEM((slots // GROUP, 8 * GROUP, wide), BF16),
            pltpu.VMEM((rows, wide), BF16),
            pltpu.SemaphoreType.DMA((slots // GROUP + 4,)),
            pltpu.SemaphoreType.DMA((slots // GROUP,)),
        ],
        compiler_params=params(0, 36),
    )(got, w_gate, w_up, w_down)
    over = exchange(over.reshape(slots, 8, wide)).reshape(rows, wide)
    main = pl.pallas_call(
        ffn_main_kernel,
        name="ffn_main",
        in_specs=[hbm] * 4,
        out_specs=hbm,
        out_shape=shape((rows, width)),
        scratch_shapes=[
            pltpu.VMEM((4, slots, 8, wide), BF16),
            pltpu.VMEM((width, hid), BF16),
            pltpu.VMEM((width, hid), BF16),
            pltpu.VMEM((hid, width), BF16),
            pltpu.VMEM((rows, hid), F32),
            pltpu.VMEM((rows, hid), F32),
            pltpu.VMEM((rows, hid), BF16),
            pltpu.VMEM((rows, width), BF16),
            pltpu.SemaphoreType.DMA((16,)),
            pltpu.SemaphoreType.DMA((4 * rows // 512,)),
        ],
        compiler_params=params(0),
    )(got, w_gate, w_up, w_down)
    main = exchange(main.reshape(slots, 8, width)).reshape(rows, width)

    total = pl.pallas_call(
        combine_over_kernel,
        name="combine_over",
        grid=(1,),
        in_specs=[whole(2 * tok, 2 * slots), whole(rows, wide)],
        out_specs=whole(tok, width),
        out_shape=shape((tok, width), F32),
        compiler_params=params(1),
    )(cover, over)
    return pl.pallas_call(
        combine_main_kernel,
        name="combine_main",
        in_specs=[hbm] * 3,
        out_specs=hbm,
        out_shape=shape((tok, width)),
        scratch_shapes=[
            pltpu.VMEM((2 * tok, rows), BF16),
            pltpu.VMEM((tok, width), F32),
            pltpu.VMEM((rows, width), BF16),
            pltpu.VMEM((tok, width), BF16),
            pltpu.SemaphoreType.DMA((len(COLUMNS),)),
            pltpu.SemaphoreType.DMA((len(COLUMNS),)),
            pltpu.SemaphoreType.DMA((len(COLUMNS),)),
            pltpu.SemaphoreType.DMA,
        ],
        compiler_params=params(0),
    )(cmain, total, main)


def solution(mesh):
    placed = (
        P(AXES, None),
        P(AXES, None),
        P(AXES, None),
        P(),
        P(AXES, None, None),
        P(AXES, None, None),
        P(AXES, None, None),
    )
    return jax.shard_map(on_device, mesh=mesh, in_specs=placed, out_specs=P(AXES, None), check_vma=False)
```

```python
import functools

import jax
import jax.numpy as jnp
from jax import lax
from jax.experimental import pallas as pl
from jax.experimental.pallas import tpu as pltpu
from jax.sharding import PartitionSpec as P


AXES = ("node", "local")
F32 = jnp.float32
BF16 = jnp.bfloat16


def iota(shape, dim):
    return lax.broadcasted_iota(jnp.int32, shape, dim)


def dot(a, b):
    return jnp.dot(a, b, preferred_element_type=F32)


def rank_by_slot(routes_t, place_row):
    top, tok = routes_t.shape
    slots = place_row.shape[1]
    rows = iota((slots, tok), 0)
    chosen = jnp.zeros((slots, tok), F32)
    for k in range(top):
        chosen = chosen + (routes_t[k : k + 1, :] == rows).astype(F32)
    perm = (place_row == iota((slots, slots), 0)).astype(F32).astype(BF16)
    at_slot = dot(perm, chosen.astype(BF16))
    before = (iota((tok, tok), 0) < iota((tok, tok), 1)).astype(F32).astype(BF16)
    rank = dot(at_slot.astype(BF16), before)
    return jnp.where(at_slot > 0.5, rank, -1.0)


GROUP = 32


def regroup(back):
    size = GROUP * 8
    grouped, plain = iota((size, size), 1 if back else 0), iota((size, size), 0 if back else 1)
    return (plain == grouped % GROUP * 8 + grouped // GROUP).astype(F32).astype(BF16)


class Queue:
    def __init__(self, copies, depth):
        self.copies, self.depth, self.done = copies, depth, 0
        for copy in copies[:depth]:
            copy.start()

    def next(self):
        self.copies[self.done].wait()
        self.done += 1
        if self.done + self.depth <= len(self.copies):
            self.copies[self.done + self.depth - 1].start()


def pack_kernel(routes_ref, place_ref, tok_ref, out_ref, part_ref):
    tok, width = tok_ref.shape
    slots = place_ref.shape[1]
    groups = slots // GROUP
    wide = width // 4
    pair = GROUP * 2
    key = rank_by_slot(routes_ref[...], place_ref[...])
    hit = key[:, None, :] == iota((slots, 8, tok), 1).astype(F32)
    sel = hit.astype(F32).reshape(slots * 8, tok).astype(BF16)

    def send(q, lo, hi, value):
        out_ref[lo:hi, q * 8 : (q + 1) * 8, :] = value.reshape(hi - lo, 8, wide).astype(BF16)

    half = slots // 2
    for q in range(4):
        for lo in (0, half):
            rows = sel[lo * 8 : (lo + half) * 8]
            send(q, lo, lo + half, dot(rows, tok_ref[:, q * wide : (q + 1) * wide]))
    sel = jnp.concatenate(
        [
            (key[g * GROUP : (g + 1) * GROUP, :] == 8.0 + r).astype(F32)
            for g in range(groups)
            for r in range(2)
        ],
        axis=0,
    ).astype(BF16)
    for q in range(4):
        out = dot(sel, tok_ref[:, q * wide : (q + 1) * wide]).astype(BF16)
        for g in range(groups):
            part_ref[g, q * pair : (q + 1) * pair, :] = out[g * pair : (g + 1) * pair]
    order = regroup(True)
    for g in range(groups):
        send(4, g * GROUP, (g + 1) * GROUP, dot(order, part_ref[g]))


def silu_mul(gate, up):
    return (gate / (1.0 + jnp.exp(-gate)) * up).astype(BF16)


def ffn_main_kernel(
    got_ref,
    wg_hbm,
    wu_hbm,
    wd_hbm,
    out_ref,
    x_ref,
    wg_ref,
    wu_ref,
    wd_ref,
    gate_ref,
    up_ref,
    hid_ref,
    back_ref,
    in_sems,
    out_sems,
):
    rows, width = back_ref.shape
    wide = width // 4
    block = 512
    blocks = [slice(m, m + block) for m in range(0, rows, block)]
    quarters = [slice(q * wide, (q + 1) * wide) for q in range(4)]
    sem = iter(range(16))
    copies = []
    for q, p in enumerate(quarters):
        copies.append(pltpu.make_async_copy(got_ref.at[:, 8 * q : 8 * q + 8, :], x_ref.at[q], in_sems.at[next(sem)]))
        copies.append(pltpu.make_async_copy(wg_hbm.at[0, p, :], wg_ref.at[p, :], in_sems.at[next(sem)]))
        copies.append(pltpu.make_async_copy(wu_hbm.at[0, p, :], wu_ref.at[p, :], in_sems.at[next(sem)]))
    for p in quarters:
        copies.append(pltpu.make_async_copy(wd_hbm.at[0, :, p], wd_ref.at[:, p], in_sems.at[next(sem)]))
    queue = Queue(copies, 5)
    for q, p in enumerate(quarters):
        for _ in range(3):
            queue.next()
        for m in blocks:
            x = x_ref[q, m.start // 8 : m.stop // 8].reshape(block, wide)
            gate = dot(x, wg_ref[p, :])
            up = dot(x, wu_ref[p, :])
            if q:
                gate = gate + gate_ref[m, :]
                up = up + up_ref[m, :]
            if q < 3:
                gate_ref[m, :] = gate
                up_ref[m, :] = up
            else:
                hid_ref[m, :] = silu_mul(gate, up)
    give = []
    for p in quarters:
        queue.next()
        for m in blocks:
            back_ref[m, p] = dot(hid_ref[m, :], wd_ref[:, p]).astype(BF16)
            copy = pltpu.make_async_copy(back_ref.at[m, p], out_ref.at[m, p], out_sems.at[len(give)])
            copy.start()
            give.append(copy)
    for copy in give:
        copy.wait()


def ffn_over_kernel(
    got_ref, wg_ref, wu_ref, wd_hbm, out_ref, x_ref, wd_ref, part_ref, back_ref, in_sems, out_sems
):
    groups = part_ref.shape[0]
    wide = x_ref.shape[2]
    size = GROUP * 8
    pair = GROUP * 2
    quarters = [slice(q * wide, (q + 1) * wide) for q in range(4)]
    slots = [slice(g * GROUP, (g + 1) * GROUP) for g in range(groups)]
    lines = [slice(g * size, (g + 1) * size) for g in range(groups)]
    take = [pltpu.make_async_copy(got_ref.at[s, 32:40, :], x_ref.at[s], in_sems.at[g]) for g, s in enumerate(slots)]
    give = [pltpu.make_async_copy(back_ref.at[r, :], out_ref.at[r, :], out_sems.at[g]) for g, r in enumerate(lines)]
    downs = [
        pltpu.make_async_copy(wd_hbm.at[0, :, p], wd_ref.at[:, p], in_sems.at[groups + q]) for q, p in enumerate(quarters)
    ]
    queue = Queue(take + downs, 5)
    order = regroup(False)
    for g in range(groups):
        queue.next()
        part_ref[g] = dot(order, x_ref[slots[g]].reshape(size, wide)).astype(BF16)
    gate = up = None
    for q, p in enumerate(quarters):
        x = jnp.concatenate([part_ref[g, q * pair : (q + 1) * pair, :] for g in range(groups)], axis=0)
        one = dot(x, wg_ref[0, p, :])
        two = dot(x, wu_ref[0, p, :])
        gate, up = (one, two) if q == 0 else (gate + one, up + two)
    hidden = silu_mul(gate, up)
    for q, p in enumerate(quarters):
        queue.next()
        out = dot(hidden, wd_ref[:, p]).astype(BF16)
        for g in range(groups):
            part_ref[g, q * pair : (q + 1) * pair, :] = out[g * pair : (g + 1) * pair]
    order = regroup(True)
    for g in range(groups):
        back_ref[lines[g], :] = dot(order, part_ref[g]).astype(BF16)
        give[g].start()
    for copy in give:
        copy.wait()


def weights_kernel(routes_ref, gates_ref, place_ref, cmain_ref, cover_ref):
    tok, top = routes_ref.shape
    slots = place_ref.shape[0]
    lanes = iota((tok, slots), 1)
    chosen = jnp.zeros((tok, slots), F32)
    weight = jnp.zeros((tok, slots), F32)
    for k in range(top):
        hit = (routes_ref[:, k : k + 1] == lanes).astype(F32)
        chosen = chosen + hit
        weight = weight + hit * gates_ref[:, k : k + 1]
    perm = (place_ref[...] == iota((slots, slots), 1)).astype(F32).astype(BF16)
    high = weight.astype(BF16)
    low = (weight - high.astype(F32)).astype(BF16)
    at_slot = dot(chosen.astype(BF16), perm)
    before = (iota((tok, tok), 1) < iota((tok, tok), 0)).astype(F32).astype(BF16)
    rank = dot(before, at_slot.astype(BF16))
    key = jnp.where(at_slot > 0.5, rank, -1.0).astype(BF16)
    high = dot(high, perm).astype(BF16)
    low = dot(low, perm).astype(BF16)

    def place(out_ref, slot_of, rank_of):
        width = out_ref.shape[1]
        lane = iota((slots, width), 1)
        spread = (slot_of(lane) == iota((slots, width), 0)).astype(F32).astype(BF16)
        hit = dot(key, spread) == rank_of(iota((tok, width), 1)).astype(F32)
        out_ref[:tok, :] = jnp.where(hit, dot(high, spread), 0.0).astype(BF16)
        out_ref[tok:, :] = jnp.where(hit, dot(low, spread), 0.0).astype(BF16)

    place(cmain_ref, lambda i: i // 8, lambda i: i % 8)
    place(cover_ref, lambda i: i // (2 * GROUP) * GROUP + i % GROUP, lambda i: 8 + i // GROUP % 2)


def combine_kernel(cmain_ref, cover_ref, over_hbm, main_ref, out_ref, over_ref, early_ref, y_ref, over_sem, sems):
    tok, _ = y_ref.shape
    wide = over_ref.shape[1]
    size = GROUP * 8
    pair = GROUP * 2
    quarters = [slice(q * wide, (q + 1) * wide) for q in range(4)]
    fetch = pltpu.make_async_copy(over_hbm, over_ref, over_sem)
    fetch.start()
    for q in range(2):
        early_ref[q] = dot(cmain_ref[...], main_ref[:, quarters[q]])
    fetch.wait()
    order = regroup(False)
    parts = [dot(order, over_ref[i : i + size, :]).astype(BF16) for i in range(0, over_ref.shape[0], size)]
    copies = []
    for q, p in enumerate(quarters):
        total = early_ref[q] if q < 2 else dot(cmain_ref[...], main_ref[:, p])
        over = jnp.concatenate([part[q * pair : (q + 1) * pair] for part in parts], axis=0)
        total = total + dot(cover_ref[...], over)
        y_ref[:, p] = (total[:tok] + total[tok:]).astype(BF16)
        copy = pltpu.make_async_copy(y_ref.at[:, p], out_ref.at[:, p], sems.at[q])
        copy.start()
        copies.append(copy)
    for copy in copies:
        copy.wait()


def params(grid_dims, mib=60):
    return pltpu.CompilerParams(dimension_semantics=("arbitrary",) * grid_dims if grid_dims else None, vmem_limit_bytes=mib << 20)


def shape(dims, kind=BF16):
    return jax.ShapeDtypeStruct(dims, kind)


def on_device(tokens, routes, gates, placement, w_gate, w_up, w_down):
    tok, width = tokens.shape
    slots = placement.shape[0]
    hid = w_gate.shape[2]
    rows = slots * 8
    wide = width // 4
    exchange = functools.partial(lax.all_to_all, axis_name=AXES, split_axis=0, concat_axis=0, tiled=True)
    whole = lambda *dims: pl.BlockSpec(dims, lambda *_: (0,) * len(dims))

    hbm = pl.BlockSpec(memory_space=pl.ANY)
    vmem = pl.BlockSpec(memory_space=pltpu.VMEM)
    sent = pl.pallas_call(
        pack_kernel,
        name="pack",
        in_specs=[vmem, vmem, vmem],
        out_specs=vmem,
        out_shape=pltpu.VMEM((slots, 40, wide), BF16),
        scratch_shapes=[pltpu.VMEM((slots // GROUP, 8 * GROUP, wide), BF16)],
        compiler_params=params(0, 48),
    )(routes.T, placement.reshape(1, slots), tokens)
    got = exchange(sent)
    cmain, cover = pl.pallas_call(
        weights_kernel,
        name="weights",
        grid=(1,),
        in_specs=[whole(tok, routes.shape[1]), whole(tok, routes.shape[1]), whole(slots, 1)],
        out_specs=[whole(2 * tok, rows), whole(2 * tok, 2 * slots)],
        out_shape=[shape((2 * tok, rows)), shape((2 * tok, 2 * slots))],
        compiler_params=params(1),
    )(routes, gates, placement.reshape(slots, 1))

    over = pl.pallas_call(
        ffn_over_kernel,
        name="ffn_over",
        in_specs=[hbm, vmem, vmem, hbm],
        out_specs=hbm,
        out_shape=shape((rows, wide)),
        scratch_shapes=[
            pltpu.VMEM((slots, 8, wide), BF16),
            pltpu.VMEM((hid, width), BF16),
            pltpu.VMEM((slots // GROUP, 8 * GROUP, wide), BF16),
            pltpu.VMEM((rows, wide), BF16),
            pltpu.SemaphoreType.DMA((slots // GROUP + 4,)),
            pltpu.SemaphoreType.DMA((slots // GROUP,)),
        ],
        compiler_params=params(0, 36),
    )(got, w_gate, w_up, w_down)
    over = exchange(over.reshape(slots, 8, wide)).reshape(rows, wide)
    main = pl.pallas_call(
        ffn_main_kernel,
        name="ffn_main",
        in_specs=[hbm] * 4,
        out_specs=hbm,
        out_shape=shape((rows, width)),
        scratch_shapes=[
            pltpu.VMEM((4, slots, 8, wide), BF16),
            pltpu.VMEM((width, hid), BF16),
            pltpu.VMEM((width, hid), BF16),
            pltpu.VMEM((hid, width), BF16),
            pltpu.VMEM((rows, hid), F32),
            pltpu.VMEM((rows, hid), F32),
            pltpu.VMEM((rows, hid), BF16),
            pltpu.VMEM((rows, width), BF16),
            pltpu.SemaphoreType.DMA((16,)),
            pltpu.SemaphoreType.DMA((4 * rows // 512,)),
        ],
        compiler_params=params(0, 63),
    )(got, w_gate, w_up, w_down)
    main = exchange(main.reshape(slots, 8, width)).reshape(rows, width)

    return pl.pallas_call(
        combine_kernel,
        name="combine",
        in_specs=[vmem, vmem, hbm, vmem],
        out_specs=hbm,
        out_shape=shape((tok, width)),
        scratch_shapes=[
            pltpu.VMEM((rows, wide), BF16),
            pltpu.VMEM((2, 2 * tok, wide), F32),
            pltpu.VMEM((tok, width), BF16),
            pltpu.SemaphoreType.DMA,
            pltpu.SemaphoreType.DMA((4,)),
        ],
        compiler_params=params(0, 32),
    )(cmain, cover, over, main)


def solution(mesh):
    placed = (
        P(AXES, None),
        P(AXES, None),
        P(AXES, None),
        P(),
        P(AXES, None, None),
        P(AXES, None, None),
        P(AXES, None, None),
    )
    return jax.shard_map(on_device, mesh=mesh, in_specs=placed, out_specs=P(AXES, None), check_vma=False)
```

```python
import functools

import jax
import jax.numpy as jnp
from jax import lax
from jax.experimental import pallas as pl
from jax.experimental.pallas import tpu as pltpu
from jax.sharding import PartitionSpec as P


AXES = ("node", "local")
F32 = jnp.float32
BF16 = jnp.bfloat16


def iota(shape, dim):
    return lax.broadcasted_iota(jnp.int32, shape, dim)


def dot(a, b):
    return jnp.dot(a, b, preferred_element_type=F32)


def rank_by_slot(routes_t, place_row):
    top, tok = routes_t.shape
    slots = place_row.shape[1]
    rows = iota((slots, tok), 0)
    chosen = jnp.zeros((slots, tok), F32)
    for k in range(top):
        chosen = chosen + (routes_t[k : k + 1, :] == rows).astype(F32)
    perm = (place_row == iota((slots, slots), 0)).astype(F32).astype(BF16)
    at_slot = dot(perm, chosen.astype(BF16))
    before = (iota((tok, tok), 0) < iota((tok, tok), 1)).astype(F32).astype(BF16)
    rank = dot(at_slot.astype(BF16), before)
    return jnp.where(at_slot > 0.5, rank, -1.0)


GROUP = 32


def regroup(back):
    size = GROUP * 8
    grouped, plain = iota((size, size), 1 if back else 0), iota((size, size), 0 if back else 1)
    return (plain == grouped % GROUP * 8 + grouped // GROUP).astype(F32).astype(BF16)


class Queue:
    def __init__(self, copies, depth):
        self.copies, self.depth, self.done = copies, depth, 0
        for copy in copies[:depth]:
            copy.start()

    def next(self):
        self.copies[self.done].wait()
        self.done += 1
        if self.done + self.depth <= len(self.copies):
            self.copies[self.done + self.depth - 1].start()


def pack_kernel(routes_ref, place_ref, tok_ref, out_ref, part_ref):
    tok, width = tok_ref.shape
    slots = place_ref.shape[1]
    groups = slots // GROUP
    wide = width // 4
    pair = GROUP * 2
    key = rank_by_slot(routes_ref[...], place_ref[...])
    hit = key[:, None, :] == iota((slots, 8, tok), 1).astype(F32)
    sel = hit.astype(F32).reshape(slots * 8, tok).astype(BF16)

    def send(q, lo, hi, value):
        out_ref[lo:hi, q * 8 : (q + 1) * 8, :] = value.reshape(hi - lo, 8, wide).astype(BF16)

    half = slots // 2
    for q in range(4):
        for lo in (0, half):
            rows = sel[lo * 8 : (lo + half) * 8]
            send(q, lo, lo + half, dot(rows, tok_ref[:, q * wide : (q + 1) * wide]))
    sel = jnp.concatenate(
        [
            (key[g * GROUP : (g + 1) * GROUP, :] == 8.0 + r).astype(F32)
            for g in range(groups)
            for r in range(2)
        ],
        axis=0,
    ).astype(BF16)
    for q in range(4):
        out = dot(sel, tok_ref[:, q * wide : (q + 1) * wide]).astype(BF16)
        for g in range(groups):
            part_ref[g, q * pair : (q + 1) * pair, :] = out[g * pair : (g + 1) * pair]
    order = regroup(True)
    for g in range(groups):
        send(4, g * GROUP, (g + 1) * GROUP, dot(order, part_ref[g]))


def silu_mul(gate, up):
    return (gate / (1.0 + jnp.exp(-gate)) * up).astype(BF16)


def ffn_main_kernel(
    got_ref,
    wg_hbm,
    wu_hbm,
    wd_hbm,
    out_ref,
    x_ref,
    wg_ref,
    wu_ref,
    wd_ref,
    gate_ref,
    up_ref,
    hid_ref,
    back_ref,
    in_sems,
    out_sems,
):
    rows, width = back_ref.shape
    wide = width // 4
    block = 512
    blocks = [slice(m, m + block) for m in range(0, rows, block)]
    quarters = [slice(q * wide, (q + 1) * wide) for q in range(4)]
    sem = iter(range(16))
    copies = []
    for q, p in enumerate(quarters):
        copies.append(pltpu.make_async_copy(got_ref.at[:, 8 * q : 8 * q + 8, :], x_ref.at[q], in_sems.at[next(sem)]))
        copies.append(pltpu.make_async_copy(wg_hbm.at[0, p, :], wg_ref.at[p, :], in_sems.at[next(sem)]))
        copies.append(pltpu.make_async_copy(wu_hbm.at[0, p, :], wu_ref.at[p, :], in_sems.at[next(sem)]))
    for p in quarters:
        copies.append(pltpu.make_async_copy(wd_hbm.at[0, :, p], wd_ref.at[:, p], in_sems.at[next(sem)]))
    queue = Queue(copies, 5)
    for q, p in enumerate(quarters):
        for _ in range(3):
            queue.next()
        for m in blocks:
            x = x_ref[q, m.start // 8 : m.stop // 8].reshape(block, wide)
            gate = dot(x, wg_ref[p, :])
            up = dot(x, wu_ref[p, :])
            if q:
                gate = gate + gate_ref[m, :]
                up = up + up_ref[m, :]
            if q < 3:
                gate_ref[m, :] = gate
                up_ref[m, :] = up
            else:
                hid_ref[m, :] = silu_mul(gate, up)
    give = []
    for p in quarters:
        queue.next()
        for m in blocks:
            back_ref[m, p] = dot(hid_ref[m, :], wd_ref[:, p]).astype(BF16)
            copy = pltpu.make_async_copy(back_ref.at[m, p], out_ref.at[m, p], out_sems.at[len(give)])
            copy.start()
            give.append(copy)
    for copy in give:
        copy.wait()


def ffn_over_kernel(
    got_ref, wg_ref, wu_ref, wd_ref, out_ref, x_ref, part_ref, back_ref, in_sems, out_sems
):
    groups = part_ref.shape[0]
    wide = x_ref.shape[2]
    size = GROUP * 8
    pair = GROUP * 2
    quarters = [slice(q * wide, (q + 1) * wide) for q in range(4)]
    slots = [slice(g * GROUP, (g + 1) * GROUP) for g in range(groups)]
    lines = [slice(g * size, (g + 1) * size) for g in range(groups)]
    take = [pltpu.make_async_copy(got_ref.at[s, 32:40, :], x_ref.at[s], in_sems.at[g]) for g, s in enumerate(slots)]
    give = [pltpu.make_async_copy(back_ref.at[r, :], out_ref.at[r, :], out_sems.at[g]) for g, r in enumerate(lines)]
    queue = Queue(take, 4)
    order = regroup(False)
    for g in range(groups):
        queue.next()
        part_ref[g] = dot(order, x_ref[slots[g]].reshape(size, wide)).astype(BF16)
    gate = up = None
    for q, p in enumerate(quarters):
        x = jnp.concatenate([part_ref[g, q * pair : (q + 1) * pair, :] for g in range(groups)], axis=0)
        one = dot(x, wg_ref[0, p, :])
        two = dot(x, wu_ref[0, p, :])
        gate, up = (one, two) if q == 0 else (gate + one, up + two)
    hidden = silu_mul(gate, up)
    for q, p in enumerate(quarters):
        out = dot(hidden, wd_ref[0, :, p]).astype(BF16)
        for g in range(groups):
            part_ref[g, q * pair : (q + 1) * pair, :] = out[g * pair : (g + 1) * pair]
    order = regroup(True)
    for g in range(groups):
        back_ref[lines[g], :] = dot(order, part_ref[g]).astype(BF16)
        give[g].start()
    for copy in give:
        copy.wait()


def weights_kernel(routes_ref, gates_ref, place_ref, cmain_ref, cover_ref):
    tok, top = routes_ref.shape
    slots = place_ref.shape[0]
    lanes = iota((tok, slots), 1)
    chosen = jnp.zeros((tok, slots), F32)
    weight = jnp.zeros((tok, slots), F32)
    for k in range(top):
        hit = (routes_ref[:, k : k + 1] == lanes).astype(F32)
        chosen = chosen + hit
        weight = weight + hit * gates_ref[:, k : k + 1]
    perm = (place_ref[...] == iota((slots, slots), 1)).astype(F32).astype(BF16)
    high = weight.astype(BF16)
    low = (weight - high.astype(F32)).astype(BF16)
    at_slot = dot(chosen.astype(BF16), perm)
    before = (iota((tok, tok), 1) < iota((tok, tok), 0)).astype(F32).astype(BF16)
    rank = dot(before, at_slot.astype(BF16))
    key = jnp.where(at_slot > 0.5, rank, -1.0).astype(BF16)
    high = dot(high, perm).astype(BF16)
    low = dot(low, perm).astype(BF16)

    def place(out_ref, slot_of, rank_of):
        width = out_ref.shape[1]
        lane = iota((slots, width), 1)
        spread = (slot_of(lane) == iota((slots, width), 0)).astype(F32).astype(BF16)
        hit = dot(key, spread) == rank_of(iota((tok, width), 1)).astype(F32)
        out_ref[:tok, :] = jnp.where(hit, dot(high, spread), 0.0).astype(BF16)
        out_ref[tok:, :] = jnp.where(hit, dot(low, spread), 0.0).astype(BF16)

    place(cmain_ref, lambda i: i // 8, lambda i: i % 8)
    place(cover_ref, lambda i: i // (2 * GROUP) * GROUP + i % GROUP, lambda i: 8 + i // GROUP % 2)


def combine_kernel(cmain_ref, cover_ref, over_hbm, main_ref, out_ref, over_ref, early_ref, y_ref, over_sem, sems):
    tok, _ = y_ref.shape
    wide = over_ref.shape[1]
    size = GROUP * 8
    pair = GROUP * 2
    quarters = [slice(q * wide, (q + 1) * wide) for q in range(4)]
    fetch = pltpu.make_async_copy(over_hbm, over_ref, over_sem)
    fetch.start()
    for q in range(2):
        early_ref[q] = dot(cmain_ref[...], main_ref[:, quarters[q]])
    fetch.wait()
    order = regroup(False)
    parts = [dot(order, over_ref[i : i + size, :]).astype(BF16) for i in range(0, over_ref.shape[0], size)]
    copies = []
    for q, p in enumerate(quarters):
        total = early_ref[q] if q < 2 else dot(cmain_ref[...], main_ref[:, p])
        over = jnp.concatenate([part[q * pair : (q + 1) * pair] for part in parts], axis=0)
        total = total + dot(cover_ref[...], over)
        y_ref[:, p] = (total[:tok] + total[tok:]).astype(BF16)
        copy = pltpu.make_async_copy(y_ref.at[:, p], out_ref.at[:, p], sems.at[q])
        copy.start()
        copies.append(copy)
    for copy in copies:
        copy.wait()


def params(grid_dims, mib=60):
    return pltpu.CompilerParams(dimension_semantics=("arbitrary",) * grid_dims if grid_dims else None, vmem_limit_bytes=mib << 20)


def shape(dims, kind=BF16):
    return jax.ShapeDtypeStruct(dims, kind)


def on_device(tokens, routes, gates, placement, w_gate, w_up, w_down):
    tok, width = tokens.shape
    slots = placement.shape[0]
    hid = w_gate.shape[2]
    rows = slots * 8
    wide = width // 4
    exchange = functools.partial(lax.all_to_all, axis_name=AXES, split_axis=0, concat_axis=0, tiled=True)
    whole = lambda *dims: pl.BlockSpec(dims, lambda *_: (0,) * len(dims))

    hbm = pl.BlockSpec(memory_space=pl.ANY)
    vmem = pl.BlockSpec(memory_space=pltpu.VMEM)
    sent = pl.pallas_call(
        pack_kernel,
        name="pack",
        in_specs=[vmem, vmem, vmem],
        out_specs=vmem,
        out_shape=pltpu.VMEM((slots, 40, wide), BF16),
        scratch_shapes=[pltpu.VMEM((slots // GROUP, 8 * GROUP, wide), BF16)],
        compiler_params=params(0, 48),
    )(routes.T, placement.reshape(1, slots), tokens)
    got = exchange(sent)
    cmain, cover = pl.pallas_call(
        weights_kernel,
        name="weights",
        grid=(1,),
        in_specs=[whole(tok, routes.shape[1]), whole(tok, routes.shape[1]), whole(slots, 1)],
        out_specs=[whole(2 * tok, rows), whole(2 * tok, 2 * slots)],
        out_shape=[shape((2 * tok, rows)), shape((2 * tok, 2 * slots))],
        compiler_params=params(1),
    )(routes, gates, placement.reshape(slots, 1))

    over = pl.pallas_call(
        ffn_over_kernel,
        name="ffn_over",
        in_specs=[hbm, vmem, vmem, vmem],
        out_specs=hbm,
        out_shape=shape((rows, wide)),
        scratch_shapes=[
            pltpu.VMEM((slots, 8, wide), BF16),
            pltpu.VMEM((slots // GROUP, 8 * GROUP, wide), BF16),
            pltpu.VMEM((rows, wide), BF16),
            pltpu.SemaphoreType.DMA((slots // GROUP,)),
            pltpu.SemaphoreType.DMA((slots // GROUP,)),
        ],
        compiler_params=params(0, 20),
    )(got, w_gate, w_up, w_down)
    over = exchange(over.reshape(slots, 8, wide)).reshape(rows, wide)
    main = pl.pallas_call(
        ffn_main_kernel,
        name="ffn_main",
        in_specs=[hbm] * 4,
        out_specs=hbm,
        out_shape=shape((rows, width)),
        scratch_shapes=[
            pltpu.VMEM((4, slots, 8, wide), BF16),
            pltpu.VMEM((width, hid), BF16),
            pltpu.VMEM((width, hid), BF16),
            pltpu.VMEM((hid, width), BF16),
            pltpu.VMEM((rows, hid), F32),
            pltpu.VMEM((rows, hid), F32),
            pltpu.VMEM((rows, hid), BF16),
            pltpu.VMEM((rows, width), BF16),
            pltpu.SemaphoreType.DMA((16,)),
            pltpu.SemaphoreType.DMA((4 * rows // 512,)),
        ],
        compiler_params=params(0, 63),
    )(got, w_gate, w_up, w_down)
    main = exchange(main.reshape(slots, 8, width)).reshape(rows, width)

    return pl.pallas_call(
        combine_kernel,
        name="combine",
        in_specs=[vmem, vmem, hbm, vmem],
        out_specs=hbm,
        out_shape=shape((tok, width)),
        scratch_shapes=[
            pltpu.VMEM((rows, wide), BF16),
            pltpu.VMEM((2, 2 * tok, wide), F32),
            pltpu.VMEM((tok, width), BF16),
            pltpu.SemaphoreType.DMA,
            pltpu.SemaphoreType.DMA((4,)),
        ],
        compiler_params=params(0, 32),
    )(cmain, cover, over, main)


def solution(mesh):
    placed = (
        P(AXES, None),
        P(AXES, None),
        P(AXES, None),
        P(),
        P(AXES, None, None),
        P(AXES, None, None),
        P(AXES, None, None),
    )
    return jax.shard_map(on_device, mesh=mesh, in_specs=placed, out_specs=P(AXES, None), check_vma=False)
```
